32 devices in a mesh: rep: 8 (over y, x, core), tp: 4 (over z).
Axes of the slice: x: 2, y: 2, z: 4, core: 2. Of those that a mesh axis runs over, the one named last changes fastest.
Arguments:
- tokens: bfloat16 [4096, 8192], P('rep', 'tp'), may hold values from -6 to 6
- query_weight: bfloat16 [8192, 4096], P(None, 'tp'), may hold values from -0.0625 to 0.0625
- key_value_weight: bfloat16 [8192, 1024], P('tp'), may hold values from -0.0625 to 0.0625
- adapter_down_tables: bfloat16 [32, 192, 8192], P('rep', None, 'tp'), may hold values from -0.0625 to 0.0625
- adapter_up_query: bfloat16 [32, 64, 4096], P('rep', None, 'tp'), may hold values from -0.75 to 0.75
- adapter_up_key_value: bfloat16 [32, 64, 1024], P('rep', None, 'tp'), may hold values from -0.75 to 0.75
- request_adapter: int32 [128], P('rep'), may hold values from 0 to 31, as said below
- request_token_length: int32 [128], P('rep'), may hold values from 8 to 32, as said below
- adapter_table_row: int32 [32], replicated, may hold values from 0 to 31, as said below
Outputs:
- attended: bfloat16 [4096, 4096], P('rep', 'tp')
The draws below stay inside these ranges and needn't reach their ends.
Inputs may be any that keep to these rules, and one draw needn't show every extreme that they name: `request_adapter`: in each replica's block of 16 requests at most 4 have adapters whose table rows adapter_table_row lies in one index of rep's share (rows s with the same s // 4); in every draw one share gets exactly 4 from every replica. `adapter_table_row`: A permutation of the table rows. `request_token_length`: every replica has one request of exactly 32 tokens.
All inputs are finite; a program needn't handle non-finite values.
Results may differ from the reference program's by a relative error of at most 0.0098.
Values may be sent and summed in bfloat16 or wider, within the bound.
A program may use at most 192 MiB of HBM per device.

```python
import math
import jax
import jax.numpy as jnp
from jax import lax

MODEL_WIDTH = 8192
HEAD_SIZE = 128
QUERY_HEADS = 32
KEY_VALUE_HEADS = 4
ADAPTER_RANK = 64
ADAPT_DEV = 4
REQS_DEV = 16
SEQ = 32
REQUESTS = 128
TOKENS = 4096
ADAPTER_COUNT = 32
CAP_REQ = 4


def draw_tokens(key, part):
    return jnp.clip(jax.random.normal(key, (TOKENS, MODEL_WIDTH), jnp.float32), -6.0, 6.0).astype(jnp.bfloat16)


def table_homes(key):
    return jax.random.permutation(jax.random.fold_in(key, 11), ADAPTER_COUNT).astype(jnp.int32)


def draw_adapter_table_row(key, part):
    return table_homes(key)


def draw_request_adapter(key, part):
    homes = table_homes(key)
    holder = jnp.zeros((ADAPTER_COUNT,), jnp.int32).at[homes].set(jnp.arange(ADAPTER_COUNT, dtype=jnp.int32))
    replicas = REQUESTS // REQS_DEV
    slot_total = replicas * CAP_REQ
    base_key = jax.random.fold_in(key, 23)
    busiest = jax.random.randint(jax.random.fold_in(base_key, 1), (), 0, replicas, dtype=jnp.int32)
    slot_owner = jnp.arange(slot_total, dtype=jnp.int32) // CAP_REQ

    def one_replica(replica_index):
        replica_key = jax.random.fold_in(base_key, replica_index + 2)
        order_key, shuffle_key, local_key = jax.random.split(replica_key, 3)
        ranking = jax.random.permutation(order_key, slot_total).astype(jnp.int32)
        priority = jnp.where(slot_owner == busiest, ranking - slot_total, ranking)
        chosen = jnp.argsort(priority, stable=True)[:REQS_DEV].astype(jnp.int32)
        owners = slot_owner[chosen]
        shuffle_order = jax.random.permutation(shuffle_key, REQS_DEV).astype(jnp.int32)
        owners = owners[shuffle_order]
        local_pick = jax.random.randint(local_key, (REQS_DEV,), 0, ADAPT_DEV, dtype=jnp.int32)
        return holder[owners * ADAPT_DEV + local_pick]
    picked = jax.vmap(one_replica)(jnp.arange(replicas, dtype=jnp.int32))
    return picked.reshape(REQUESTS).astype(jnp.int32)


def draw_request_token_length(key, part):
    replicas = REQUESTS // REQS_DEV
    first_key, second_key = jax.random.split(key)
    drawn = jax.random.randint(first_key, (replicas, REQS_DEV), max(1, SEQ // 4), SEQ + 1, dtype=jnp.int32)
    longest = jax.random.randint(second_key, (replicas, 1), 0, REQS_DEV, dtype=jnp.int32)
    filled = jnp.where(jnp.arange(REQS_DEV, dtype=jnp.int32)[None, :] == longest, SEQ, drawn)
    return filled.reshape(REQUESTS).astype(jnp.int32)


def levels(rng, dims, cuts, low, top_value):
    def one(axis_at, parts):
        heights = jax.random.uniform(jax.random.fold_in(jax.random.fold_in(rng, 6), axis_at), (parts,), jnp.float32, low / len(cuts), top_value / len(cuts))
        return jnp.repeat(jnp.exp(heights), dims[axis_at] // parts).reshape((-1,) + (1,) * (len(dims) - axis_at - 1))

    level = one(*cuts[0])
    for cut in cuts[1:]:
        level = level * one(*cut)
    return level


def noise(own_key, shape, width, reach, pieces=(), held_as=jnp.bfloat16):
    loudness = levels(own_key, shape, pieces, -0.22, 0.18) if pieces else 1.0
    values = jax.random.normal(own_key, shape, jnp.float32) * width * loudness
    return jnp.minimum(jnp.maximum(values, -reach), reach).astype(held_as)


def setup_inputs(seed: int = 0) -> dict:
    seeds = jax.random.split(jax.random.key(seed), 10)
    tokens = draw_tokens(jax.random.fold_in(seeds[9], 71), 0)
    query_weight = noise(seeds[1], (MODEL_WIDTH, QUERY_HEADS * HEAD_SIZE), MODEL_WIDTH ** -0.5, 0.0625, ((1, 4),))
    key_value_weight = noise(seeds[2], (MODEL_WIDTH, 2 * KEY_VALUE_HEADS * HEAD_SIZE), MODEL_WIDTH ** -0.5, 0.0625, ((0, 4),))
    adapter_down_tables = noise(seeds[3], (ADAPTER_COUNT, 3 * ADAPTER_RANK, MODEL_WIDTH), MODEL_WIDTH ** -0.5, 0.0625, ((0, 8), (2, 4)))
    adapter_up_query = noise(seeds[4], (ADAPTER_COUNT, ADAPTER_RANK, QUERY_HEADS * HEAD_SIZE), ADAPTER_RANK ** -0.5, 0.75, ((0, 8), (2, 4)))
    adapter_up_key_value = noise(seeds[5], (ADAPTER_COUNT, ADAPTER_RANK, 2 * KEY_VALUE_HEADS * HEAD_SIZE), ADAPTER_RANK ** -0.5, 0.75, ((0, 8), (2, 4)))
    request_adapter = draw_request_adapter(jax.random.fold_in(seeds[9], 71), 0)
    request_token_length = draw_request_token_length(jax.random.fold_in(seeds[9], 71), 0)
    adapter_table_row = draw_adapter_table_row(jax.random.fold_in(seeds[9], 71), 0)
    return {"tokens": tokens, "query_weight": query_weight, "key_value_weight": key_value_weight, "adapter_down_tables": adapter_down_tables, "adapter_up_query": adapter_up_query, "adapter_up_key_value": adapter_up_key_value, "request_adapter": request_adapter, "request_token_length": request_token_length, "adapter_table_row": adapter_table_row}


adapter_scale = 0.5
rope_theta = 500000.0

def rotary(values, positions):
    half_dim = values.shape[-1] // 2
    frequency = rope_theta ** (-(jnp.arange(half_dim, dtype=jnp.float32) * 2.0 / values.shape[-1]))
    angles = positions.astype(jnp.float32)[:, None] * frequency[None, :]
    cosine = jnp.cos(angles)[:, None, :]
    sine_part = jnp.sin(angles)[:, None, :]
    lower_half = values[..., :half_dim]
    upper_half = values[..., half_dim:]
    return jnp.concatenate([lower_half * cosine - upper_half * sine_part, upper_half * cosine + lower_half * sine_part], axis=-1)

def reference(tokens, query_weight, key_value_weight, adapter_down_tables, adapter_up_query, adapter_up_key_value, request_adapter, request_token_length, adapter_table_row):
    base_query = jnp.dot(tokens, query_weight, preferred_element_type=jnp.float32)
    base_pair = jnp.dot(tokens, key_value_weight, preferred_element_type=jnp.float32)
    table_rows = adapter_table_row[request_adapter].astype(jnp.int32)
    key_columns = jnp.arange(2 * KEY_VALUE_HEADS * HEAD_SIZE, dtype=jnp.int32) < KEY_VALUE_HEADS * HEAD_SIZE
    request_rows = tokens.reshape(REQUESTS, SEQ, MODEL_WIDTH)

    def one_request(inputs):
        rows_x, adapter_row_index = inputs
        down_projection_rows = lax.dynamic_index_in_dim(adapter_down_tables, adapter_row_index, 0, keepdims=False)
        query_up_weight = lax.dynamic_index_in_dim(adapter_up_query, adapter_row_index, 0, keepdims=False)
        key_value_up_weight = lax.dynamic_index_in_dim(adapter_up_key_value, adapter_row_index, 0, keepdims=False)
        shrink = lax.dot_general(rows_x, down_projection_rows, (((1,), (1,)), ((), ())), preferred_element_type=jnp.float32).astype(jnp.bfloat16)
        query_update = jnp.dot(shrink[:, :ADAPTER_RANK], query_up_weight, preferred_element_type=jnp.float32)
        key_part = jnp.dot(shrink[:, ADAPTER_RANK:2 * ADAPTER_RANK], key_value_up_weight, preferred_element_type=jnp.float32)
        value_part = jnp.dot(shrink[:, 2 * ADAPTER_RANK:], key_value_up_weight, preferred_element_type=jnp.float32)
        key_value_delta = jnp.where(key_columns[None, :], key_part, value_part)
        return (adapter_scale * jnp.concatenate([query_update, key_value_delta], axis=1)).astype(jnp.bfloat16)
    delta = lax.map(one_request, (request_rows, table_rows))
    delta = delta.reshape(TOKENS, QUERY_HEADS * HEAD_SIZE + 2 * KEY_VALUE_HEADS * HEAD_SIZE).astype(jnp.float32)
    positions = jnp.arange(TOKENS, dtype=jnp.int32) % SEQ
    query = rotary((base_query + delta[:, :QUERY_HEADS * HEAD_SIZE]).reshape(TOKENS, QUERY_HEADS, HEAD_SIZE), positions).astype(jnp.bfloat16)
    pair_raw = (base_pair + delta[:, QUERY_HEADS * HEAD_SIZE:]).astype(jnp.bfloat16)
    pair_raw = lax.optimization_barrier(pair_raw)
    keys_raw = pair_raw[:, :KEY_VALUE_HEADS * HEAD_SIZE].reshape(TOKENS, KEY_VALUE_HEADS, HEAD_SIZE)
    values = pair_raw[:, KEY_VALUE_HEADS * HEAD_SIZE:].reshape(REQUESTS, SEQ, KEY_VALUE_HEADS, HEAD_SIZE)
    keys = rotary(keys_raw.astype(jnp.float32), positions).astype(jnp.bfloat16)
    group_size = QUERY_HEADS // KEY_VALUE_HEADS
    query_full = query.astype(jnp.float32).reshape(REQUESTS, SEQ, KEY_VALUE_HEADS, group_size, HEAD_SIZE)
    keys_full = keys.astype(jnp.float32).reshape(REQUESTS, SEQ, KEY_VALUE_HEADS, HEAD_SIZE)
    scores = jnp.einsum('rqkgd,rpkd->rkgqp', query_full, keys_full) / math.sqrt(HEAD_SIZE)
    slot_pos = jnp.arange(SEQ, dtype=jnp.int32)
    allowed = (slot_pos[None, None, :] <= slot_pos[None, :, None]) & (slot_pos[None, None, :] < request_token_length[:, None, None])
    scores = jnp.where(allowed[:, None, None, :, :], scores, jnp.float32(-1e+30))
    peak = lax.optimization_barrier(jnp.max(scores, axis=-1, keepdims=True))
    weights = jnp.exp(scores - peak)
    probs = (weights / lax.optimization_barrier(jnp.sum(weights, axis=-1, keepdims=True))).astype(jnp.bfloat16)
    mixed = jnp.einsum('rkgqp,rpkd->rqkgd', probs.astype(jnp.float32), values.astype(jnp.float32))
    live = slot_pos[None, :] < request_token_length[:, None]
    mixed = jnp.where(live[:, :, None, None, None], mixed, jnp.float32(0.0))
    return mixed.astype(jnp.bfloat16).reshape(TOKENS, QUERY_HEADS * HEAD_SIZE)
```

```python
import math

import jax
import jax.numpy as jnp
import numpy as np
from jax import lax
from jax.experimental import pallas as pl
from jax.experimental.pallas import tpu as pltpu
from jax.sharding import PartitionSpec as P

HEAD_SIZE = 128
HALF = HEAD_SIZE // 2

adapter_scale = 0.5
rope_theta = 500000.0


def rope_tables(seq_len, rows):
    frequency = np.float64(rope_theta) ** (-(np.arange(HALF, dtype=np.float64) * 2.0 / HEAD_SIZE))
    angles = (np.arange(rows) % seq_len).astype(np.float64)[:, None] * frequency[None, :]
    cosine = np.concatenate([np.cos(angles), np.cos(angles)], axis=1)
    sine = np.concatenate([-np.sin(angles), np.sin(angles)], axis=1)
    return cosine.astype(np.float32), sine.astype(np.float32)


def attend_kernel(seq_len, per_block, heads_here, slots, lengths, base, pair, delta, cosine, sine, out):
    block = pl.program_id(0)
    rows = per_block * seq_len
    query_cols = heads_here * HEAD_SIZE
    picked = [slots[block * per_block + j] for j in range(per_block)]
    sizes = [lengths[block * per_block + j] for j in range(per_block)]

    def change(start, width):
        return jnp.concatenate(
            [delta[s, :, start : start + width] for s in picked], axis=0
        ).astype(jnp.float32)

    cos = cosine[...]
    sin = sine[...]

    def rotate(v):
        return (v * cos + pltpu.roll(v, HALF, 1) * sin).astype(jnp.bfloat16)

    keys_raw = (pair[:, :HEAD_SIZE] + change(query_cols, HEAD_SIZE)).astype(jnp.bfloat16)
    values = (pair[:, HEAD_SIZE:] + change(query_cols + HEAD_SIZE, HEAD_SIZE)).astype(jnp.bfloat16)
    keys = rotate(keys_raw.astype(jnp.float32))
    q_at = lax.broadcasted_iota(jnp.int32, (rows, rows), 0)
    p_at = lax.broadcasted_iota(jnp.int32, (rows, rows), 1)
    p_request = p_at // seq_len
    q_row = lax.broadcasted_iota(jnp.int32, (rows, HEAD_SIZE), 0)
    limit = jnp.zeros((rows, rows), jnp.int32)
    q_limit = jnp.zeros((rows, HEAD_SIZE), jnp.int32)
    for j in range(per_block):
        limit = jnp.where(p_request == j, sizes[j] + j * seq_len, limit)
        q_limit = jnp.where(q_row // seq_len == j, sizes[j] + j * seq_len, q_limit)
    allowed = (p_request == q_at // seq_len) & (p_at <= q_at) & (p_at < limit)
    live = q_row < q_limit
    for h in range(heads_here):
        at = h * HEAD_SIZE
        query = rotate(base[:, at : at + HEAD_SIZE] + change(at, HEAD_SIZE))
        scores = lax.dot_general(
            query, keys, (((1,), (1,)), ((), ())), preferred_element_type=jnp.float32
        ) * (1.0 / math.sqrt(HEAD_SIZE))
        scores = jnp.where(allowed, scores, jnp.float32(-1e30))
        weights = jnp.exp(scores - jnp.max(scores, axis=1, keepdims=True))
        probs = (weights / jnp.sum(weights, axis=1, keepdims=True)).astype(jnp.bfloat16)
        mixed = jnp.dot(probs, values, preferred_element_type=jnp.float32)
        out[:, at : at + HEAD_SIZE] = jnp.where(live, mixed, 0.0).astype(jnp.bfloat16)


def attend(slots, lengths, base, pair, delta, seq_len):
    tok_rows, query_cols = base.shape
    per_block = max(1, HEAD_SIZE // seq_len)
    rows = per_block * seq_len
    cosine, sine = rope_tables(seq_len, rows)
    whole = lambda shape: pl.BlockSpec(shape, lambda i, *_: (0,) * len(shape))
    part = lambda cols: pl.BlockSpec((rows, cols), lambda i, *_: (i, 0))

    def body(*refs):
        attend_kernel(seq_len, per_block, query_cols // HEAD_SIZE, *refs)

    return pl.pallas_call(
        body,
        out_shape=jax.ShapeDtypeStruct((tok_rows, query_cols), jnp.bfloat16),
        grid_spec=pltpu.PrefetchScalarGridSpec(
            num_scalar_prefetch=2,
            grid=(tok_rows // rows,),
            in_specs=[
                part(query_cols),
                part(2 * HEAD_SIZE),
                whole(delta.shape),
                whole(cosine.shape),
                whole(sine.shape),
            ],
            out_specs=part(query_cols),
        ),
        compiler_params=pltpu.CompilerParams(vmem_limit_bytes=32 << 20),
    )(slots, lengths, base, pair, delta, jnp.asarray(cosine), jnp.asarray(sine))


def shards(
    tokens,
    query_weight,
    key_value_weight,
    adapter_down_tables,
    adapter_up_query,
    adapter_up_key_value,
    request_adapter,
    request_token_length,
    adapter_table_row,
):
    replicas = lax.axis_size("rep")
    tp_count = lax.axis_size("tp")
    tp_here = lax.axis_index("tp")
    rep_here = lax.axis_index("rep")
    tok_rows, feat_local = tokens.shape
    query_cols = query_weight.shape[1]
    pair_total = key_value_weight.shape[1]
    local_rows = adapter_down_tables.shape[0]
    rank = adapter_up_query.shape[1]
    requests_here = request_adapter.shape[0]
    seq_len = tok_rows // requests_here
    capacity = max(1, 2 * requests_here // replicas)
    slot_count = replicas * capacity
    kv_heads = pair_total // (2 * HEAD_SIZE)
    sharing = tp_count // kv_heads

    everyone = lax.all_gather(request_adapter, "rep", axis=0, tiled=False)
    match = everyone[:, :, None] == jnp.arange(adapter_table_row.shape[0], dtype=jnp.int32)
    homes = jnp.sum(jnp.where(match, adapter_table_row, 0), axis=2)
    own_match = request_adapter[:, None] == jnp.arange(adapter_table_row.shape[0], dtype=jnp.int32)
    own_homes = jnp.sum(jnp.where(own_match, adapter_table_row, 0), axis=1)
    pos = jnp.arange(requests_here, dtype=jnp.int32)
    before = pos[None, :] < pos[:, None]
    own_owner = own_homes // local_rows
    own_earlier = (own_owner[:, None] == own_owner[None, :]) & before
    slot_ids = own_owner * capacity + jnp.sum(own_earlier.astype(jnp.int32), axis=1)
    slot_at = jnp.arange(slot_count, dtype=jnp.int32)
    slot_request = jnp.sum(jnp.where(slot_ids[None, :] == slot_at[:, None], pos, 0), axis=1)

    send = jnp.take(tokens.reshape(requests_here, seq_len, feat_local), slot_request, axis=0)
    received = lax.all_to_all(send, "rep", split_axis=0, concat_axis=0, tiled=True)
    received = received.reshape(slot_count * seq_len, feat_local)

    owners = homes // local_rows
    earlier = (owners[:, :, None] == owners[:, None, :]) & before[None]
    rank_in = jnp.sum(earlier.astype(jnp.int32), axis=2)
    cap_at = jnp.arange(capacity, dtype=jnp.int32)
    mine = (owners == rep_here)[:, None, :] & (rank_in[:, None, :] == cap_at[None, :, None])
    local = jnp.sum(jnp.where(mine, (homes % local_rows)[:, None, :], 0), axis=2)
    local_row = jnp.broadcast_to(
        local.reshape(slot_count, 1), (slot_count, seq_len)
    ).reshape(slot_count * seq_len, 1)

    base_pair = jnp.dot(tokens, key_value_weight, preferred_element_type=jnp.float32)
    side = kv_heads * HEAD_SIZE
    pieces = []
    for t in range(tp_count):
        at = (t // sharing) * HEAD_SIZE
        pieces.append(
            jnp.concatenate(
                [base_pair[:, at : at + HEAD_SIZE], base_pair[:, side + at : side + at + HEAD_SIZE]],
                axis=1,
            )
        )
    pair_here = lax.psum_scatter(jnp.stack(pieces), "tp", scatter_dimension=0, tiled=False)

    up_all = lax.all_gather(adapter_up_key_value, "tp", axis=2, tiled=True)
    head = tp_here // sharing
    up_key = lax.dynamic_slice_in_dim(up_all, head * HEAD_SIZE, HEAD_SIZE, 2)
    up_value = lax.dynamic_slice_in_dim(up_all, side + head * HEAD_SIZE, HEAD_SIZE, 2)

    gathered = lax.all_gather(tokens, "tp", axis=0, tiled=False)
    base_query = jnp.einsum(
        "tnf,tfc->nc",
        gathered,
        query_weight.reshape(tp_count, feat_local, query_cols),
        preferred_element_type=jnp.float32,
    )

    partial = jnp.zeros((slot_count * seq_len, 3 * rank), jnp.float32)
    for a in range(local_rows):
        one = lax.dot_general(
            received,
            adapter_down_tables[a],
            (((1,), (1,)), ((), ())),
            preferred_element_type=jnp.float32,
        )
        partial = jnp.where(local_row == a, one, partial)
    partials = lax.all_gather(partial.astype(jnp.bfloat16), "tp", axis=0, tiled=False)
    shrink = jnp.sum(partials.astype(jnp.float32), axis=0).astype(jnp.bfloat16)

    def expand(part, up):
        spread = jnp.concatenate(
            [jnp.where(local_row == a, part, jnp.bfloat16(0)) for a in range(local_rows)], axis=1
        )
        return jnp.dot(
            spread, up.reshape(local_rows * rank, up.shape[2]), preferred_element_type=jnp.float32
        )

    delta = jnp.concatenate(
        [
            expand(shrink[:, :rank], adapter_up_query),
            expand(shrink[:, rank : 2 * rank], up_key),
            expand(shrink[:, 2 * rank :], up_value),
        ],
        axis=1,
    )
    delta = (adapter_scale * delta).astype(jnp.bfloat16)
    returned = lax.all_to_all(
        delta.reshape(slot_count, seq_len, delta.shape[1]),
        "rep",
        split_axis=0,
        concat_axis=0,
        tiled=True,
    )
    return attend(slot_ids, request_token_length, base_query, pair_here, returned, seq_len)


def solution(mesh):
    placed = (
        P("rep", "tp"),
        P(None, "tp"),
        P("tp", None),
        P("rep", None, "tp"),
        P("rep", None, "tp"),
        P("rep", None, "tp"),
        P("rep"),
        P("rep"),
        P(),
    )
    return jax.shard_map(
        shards, mesh=mesh, in_specs=placed, out_specs=P("rep", "tp"), check_vma=False
    )
```

```python
import math

import jax
import jax.numpy as jnp
import numpy as np
from jax import lax
from jax.experimental import pallas as pl
from jax.experimental.pallas import tpu as pltpu
from jax.sharding import PartitionSpec as P

HEAD_SIZE = 128
HALF = HEAD_SIZE // 2
CHUNKS = 2

adapter_scale = 0.5
rope_theta = 500000.0


def rope_tables(seq_len, rows):
    frequency = np.float64(rope_theta) ** (-(np.arange(HALF, dtype=np.float64) * 2.0 / HEAD_SIZE))
    angles = (np.arange(rows) % seq_len).astype(np.float64)[:, None] * frequency[None, :]
    cosine = np.concatenate([np.cos(angles), np.cos(angles)], axis=1)
    sine = np.concatenate([-np.sin(angles), np.sin(angles)], axis=1)
    return cosine.astype(np.float32), sine.astype(np.float32)


def pick_kernel(count, wide, picks, tokens, marks, out, sems, mark_sem):
    copies = [
        pltpu.make_async_copy(tokens.at[picks[s]], out.at[s, :, pl.ds(0, wide)], sems.at[s])
        for s in range(count)
    ]
    tail = pltpu.make_async_copy(marks, out.at[:, :, pl.ds(wide, HEAD_SIZE)], mark_sem)
    for copy in copies:
        copy.start()
    tail.start()
    for copy in copies:
        copy.wait()
    tail.wait()


def pick_slots(picks, tokens, marks):
    count = picks.shape[0]
    _, seq_len, wide = tokens.shape
    anywhere = pl.BlockSpec(memory_space=pl.ANY)

    def body(*refs):
        pick_kernel(count, wide, *refs)

    return pl.pallas_call(
        body,
        out_shape=jax.ShapeDtypeStruct((count, seq_len, wide + HEAD_SIZE), tokens.dtype),
        grid_spec=pltpu.PrefetchScalarGridSpec(
            num_scalar_prefetch=1,
            grid=(1,),
            in_specs=[anywhere, anywhere],
            out_specs=anywhere,
            scratch_shapes=[pltpu.SemaphoreType.DMA((count,)), pltpu.SemaphoreType.DMA],
        ),
    )(picks, tokens, marks)


def down_project(received, down):
    rows, lanes = received.shape
    adapters, outs, wide = down.shape
    block = min(256, rows)

    def body(x, w, out):
        features = x[:, :wide]
        mark = x[:, wide : wide + 1].astype(jnp.float32)
        total = jnp.zeros((block, outs), jnp.float32)
        for a in range(adapters):
            one = lax.dot_general(
                features, w[a], (((1,), (1,)), ((), ())), preferred_element_type=jnp.float32
            )
            total = jnp.where(mark == float(a), one, total)
        out[...] = total.astype(jnp.bfloat16)

    return pl.pallas_call(
        body,
        out_shape=jax.ShapeDtypeStruct((rows, outs), jnp.bfloat16),
        grid=(rows // block,),
        in_specs=[
            pl.BlockSpec((block, lanes), lambda i: (i, 0)),
            pl.BlockSpec((adapters, outs, wide), lambda i: (0, 0, 0)),
        ],
        out_specs=pl.BlockSpec((block, outs), lambda i: (i, 0)),
        compiler_params=pltpu.CompilerParams(vmem_limit_bytes=32 << 20),
        cost_estimate=pl.CostEstimate(
            flops=2 * rows * outs * adapters * wide, bytes_accessed=9 << 20, transcendentals=0
        ),
    )(received, down)


def up_project(shrink, received, up_query, up_key, up_value):
    rows, outs = shrink.shape
    adapters, rank, query_cols = up_query.shape
    wide = received.shape[1] - HEAD_SIZE
    block = min(256, rows)
    cols = query_cols + 2 * HEAD_SIZE

    def body(low, marks, wq, wk, wv, out):
        mark = marks[:, :1].astype(jnp.float32)
        start = 0
        for side, w in enumerate((wq, wk, wv)):
            width = w.shape[2]
            part = low[:, side * rank : (side + 1) * rank].astype(jnp.float32)
            total = jnp.zeros((block, width), jnp.float32)
            for a in range(adapters):
                mine = jnp.where(mark == float(a), part, 0.0).astype(jnp.bfloat16)
                total += jnp.dot(mine, w[a], preferred_element_type=jnp.float32)
            out[:, start : start + width] = (adapter_scale * total).astype(jnp.bfloat16)
            start += width

    whole = lambda w: pl.BlockSpec(w.shape, lambda i: (0, 0, 0))
    return pl.pallas_call(
        body,
        out_shape=jax.ShapeDtypeStruct((rows, cols), jnp.bfloat16),
        grid=(rows // block,),
        in_specs=[
            pl.BlockSpec((block, outs), lambda i: (i, 0)),
            pl.BlockSpec((block, HEAD_SIZE), lambda i: (i, wide // HEAD_SIZE)),
            whole(up_query),
            whole(up_key),
            whole(up_value),
        ],
        out_specs=pl.BlockSpec((block, cols), lambda i: (i, 0)),
        compiler_params=pltpu.CompilerParams(vmem_limit_bytes=32 << 20),
        cost_estimate=pl.CostEstimate(
            flops=2 * rows * rank * adapters * cols, bytes_accessed=4 << 20, transcendentals=0
        ),
    )(shrink, received, up_query, up_key, up_value)


def attend_kernel(seq_len, per_block, heads_here, slots, lengths, base, pair, delta, cosine, sine, out):
    block = pl.program_id(0)
    rows = per_block * seq_len
    query_cols = heads_here * HEAD_SIZE
    picked = [slots[block * per_block + j] for j in range(per_block)]
    sizes = [lengths[block * per_block + j] for j in range(per_block)]

    def change(start, width):
        return jnp.concatenate(
            [delta[s, :, start : start + width] for s in picked], axis=0
        ).astype(jnp.float32)

    cos = cosine[...]
    sin = sine[...]

    def rotate(v):
        return (v * cos + pltpu.roll(v, HALF, 1) * sin).astype(jnp.bfloat16)

    sums = pair[0].astype(jnp.float32)
    for t in range(1, pair.shape[0]):
        sums += pair[t].astype(jnp.float32)
    keys_raw = (sums[:, :HEAD_SIZE] + change(query_cols, HEAD_SIZE)).astype(jnp.bfloat16)
    values = (sums[:, HEAD_SIZE:] + change(query_cols + HEAD_SIZE, HEAD_SIZE)).astype(jnp.bfloat16)
    keys = rotate(keys_raw.astype(jnp.float32))
    q_at = lax.broadcasted_iota(jnp.int32, (rows, rows), 0)
    p_at = lax.broadcasted_iota(jnp.int32, (rows, rows), 1)
    p_request = p_at // seq_len
    q_row = lax.broadcasted_iota(jnp.int32, (rows, HEAD_SIZE), 0)
    limit = jnp.zeros((rows, rows), jnp.int32)
    q_limit = jnp.zeros((rows, HEAD_SIZE), jnp.int32)
    for j in range(per_block):
        limit = jnp.where(p_request == j, sizes[j] + j * seq_len, limit)
        q_limit = jnp.where(q_row // seq_len == j, sizes[j] + j * seq_len, q_limit)
    allowed = (p_request == q_at // seq_len) & (p_at <= q_at) & (p_at < limit)
    live = q_row < q_limit
    for h in range(heads_here):
        at = h * HEAD_SIZE
        query = rotate(base[:, at : at + HEAD_SIZE] + change(at, HEAD_SIZE))
        scores = lax.dot_general(
            query, keys, (((1,), (1,)), ((), ())), preferred_element_type=jnp.float32
        ) * (1.0 / math.sqrt(HEAD_SIZE))
        scores = jnp.where(allowed, scores, jnp.float32(-1e30))
        weights = jnp.exp(scores - jnp.max(scores, axis=1, keepdims=True))
        probs = (weights / jnp.sum(weights, axis=1, keepdims=True)).astype(jnp.bfloat16)
        mixed = jnp.dot(probs, values, preferred_element_type=jnp.float32)
        out[:, at : at + HEAD_SIZE] = jnp.where(live, mixed, 0.0).astype(jnp.bfloat16)


def attend(slots, lengths, base, pair, delta, seq_len):
    tok_rows, query_cols = base.shape
    per_block = max(1, HEAD_SIZE // seq_len)
    rows = per_block * seq_len
    cosine, sine = rope_tables(seq_len, rows)
    whole = lambda shape: pl.BlockSpec(shape, lambda i, *_: (0,) * len(shape))
    part = lambda cols: pl.BlockSpec((rows, cols), lambda i, *_: (i, 0))

    def body(*refs):
        attend_kernel(seq_len, per_block, query_cols // HEAD_SIZE, *refs)

    return pl.pallas_call(
        body,
        out_shape=jax.ShapeDtypeStruct((tok_rows, query_cols), jnp.bfloat16),
        grid_spec=pltpu.PrefetchScalarGridSpec(
            num_scalar_prefetch=2,
            grid=(tok_rows // rows,),
            in_specs=[
                part(query_cols),
                pl.BlockSpec((pair.shape[0], rows, 2 * HEAD_SIZE), lambda i, *_: (0, i, 0)),
                whole(delta.shape),
                whole(cosine.shape),
                whole(sine.shape),
            ],
            out_specs=part(query_cols),
        ),
        compiler_params=pltpu.CompilerParams(vmem_limit_bytes=32 << 20),
    )(slots, lengths, base, pair, delta, jnp.asarray(cosine), jnp.asarray(sine))


def shards(
    tokens,
    query_weight,
    key_value_weight,
    adapter_down_tables,
    adapter_up_query,
    adapter_up_key_value,
    request_adapter,
    request_token_length,
    adapter_table_row,
):
    replicas = lax.axis_size("rep")
    tp_count = lax.axis_size("tp")
    tp_here = lax.axis_index("tp")
    tok_rows, feat_local = tokens.shape
    query_cols = query_weight.shape[1]
    pair_total = key_value_weight.shape[1]
    local_rows = adapter_down_tables.shape[0]
    rank = adapter_up_query.shape[1]
    requests_here = request_adapter.shape[0]
    seq_len = tok_rows // requests_here
    capacity = max(1, 2 * requests_here // replicas)
    slot_count = replicas * capacity
    kv_heads = pair_total // (2 * HEAD_SIZE)
    sharing = tp_count // kv_heads

    match = request_adapter[:, None] == jnp.arange(adapter_table_row.shape[0], dtype=jnp.int32)
    homes = jnp.sum(jnp.where(match, adapter_table_row[None, :], 0), axis=1)
    owners = homes // local_rows
    pos = jnp.arange(requests_here, dtype=jnp.int32)
    earlier = (owners[:, None] == owners[None, :]) & (pos[None, :] < pos[:, None])
    slot_ids = owners * capacity + jnp.sum(earlier.astype(jnp.int32), axis=1)
    slot_at = jnp.arange(slot_count, dtype=jnp.int32)
    taken = slot_ids[None, :] == slot_at[:, None]
    picks = jnp.sum(jnp.where(taken, pos, 0), axis=1)
    slot_local = jnp.sum(jnp.where(taken, (homes % local_rows)[None, :], 0), axis=1)
    marks = jnp.broadcast_to(
        slot_local.astype(jnp.bfloat16)[:, None, None], (slot_count, seq_len, HEAD_SIZE)
    )

    send = pick_slots(picks, tokens.reshape(requests_here, seq_len, feat_local), marks)
    received = lax.all_to_all(send, "rep", split_axis=0, concat_axis=0, tiled=True)
    received = received.reshape(slot_count * seq_len, feat_local + HEAD_SIZE)

    base_pair = jnp.dot(tokens, key_value_weight, preferred_element_type=jnp.float32)
    base_pair = base_pair.astype(jnp.bfloat16)
    side = kv_heads * HEAD_SIZE
    portion = adapter_up_key_value.shape[2]
    flat_up = adapter_up_key_value.reshape(local_rows * rank, portion)
    fold = local_rows * rank // 2
    pieces = []
    for t in range(tp_count):
        at = (t // sharing) * HEAD_SIZE
        up = flat_up[:, at % portion : at % portion + HEAD_SIZE]
        pieces.append(
            jnp.concatenate(
                [
                    jnp.concatenate([base_pair[:, at : at + HEAD_SIZE], up[:fold]], axis=0),
                    jnp.concatenate(
                        [base_pair[:, side + at : side + at + HEAD_SIZE], up[fold:]], axis=0
                    ),
                ],
                axis=1,
            )
        )
    swapped = lax.all_to_all(jnp.stack(pieces), "tp", split_axis=0, concat_axis=0, tiled=True)
    head = tp_here // sharing

    def up_of(column):
        both = lax.dynamic_index_in_dim(swapped, column // portion, 0, keepdims=False)[tok_rows:]
        both = jnp.concatenate([both[:, :HEAD_SIZE], both[:, HEAD_SIZE:]], axis=0)
        return both.reshape(local_rows, rank, HEAD_SIZE)

    up_key = up_of(head * HEAD_SIZE)
    up_value = up_of(side + head * HEAD_SIZE)

    chunk_rows = tok_rows // CHUNKS
    weight = query_weight.reshape(tp_count, feat_local, query_cols)
    bases = []
    for c in range(CHUNKS):
        gathered = lax.all_gather(
            tokens[c * chunk_rows : (c + 1) * chunk_rows], "tp", axis=0, tiled=False
        )
        bases.append(
            jnp.einsum("tnf,tfc->nc", gathered, weight, preferred_element_type=jnp.float32)
        )
    base_query = jnp.concatenate(bases, axis=0)

    partial = down_project(received, adapter_down_tables)
    partial = partial.reshape(tp_count, slot_count * seq_len // tp_count, 3 * rank)
    parts = lax.all_to_all(partial, "tp", split_axis=0, concat_axis=0, tiled=True)
    total = parts[0].astype(jnp.float32)
    for t in range(1, tp_count):
        total = total + parts[t].astype(jnp.float32)
    own = jnp.broadcast_to(total.astype(jnp.bfloat16)[None], partial.shape)
    shrink = lax.all_to_all(own, "tp", split_axis=0, concat_axis=0, tiled=True)
    shrink = shrink.reshape(slot_count * seq_len, 3 * rank)

    delta = up_project(shrink, received, adapter_up_query, up_key, up_value)
    returned = lax.all_to_all(
        delta.reshape(slot_count, seq_len, delta.shape[1]),
        "rep",
        split_axis=0,
        concat_axis=0,
        tiled=True,
    )
    return attend(slot_ids, request_token_length, base_query, swapped, returned, seq_len)


def solution(mesh):
    placed = (
        P("rep", "tp"),
        P(None, "tp"),
        P("tp", None),
        P("rep", None, "tp"),
        P("rep", None, "tp"),
        P("rep", None, "tp"),
        P("rep"),
        P("rep"),
        P(),
    )
    return jax.shard_map(
        shards, mesh=mesh, in_specs=placed, out_specs=P("rep", "tp"), check_vma=False
    )
```

```python
import math

import jax
import jax.numpy as jnp
import numpy as np
from jax import lax
from jax.experimental import pallas as pl
from jax.experimental.pallas import tpu as pltpu
from jax.sharding import PartitionSpec as P

HEAD_SIZE = 128
HALF = HEAD_SIZE // 2

adapter_scale = 0.5
rope_theta = 500000.0


def rope_tables(seq_len, rows):
    frequency = np.float64(rope_theta) ** (-(np.arange(HALF, dtype=np.float64) * 2.0 / HEAD_SIZE))
    angles = (np.arange(rows) % seq_len).astype(np.float64)[:, None] * frequency[None, :]
    cosine = np.concatenate([np.cos(angles), np.cos(angles)], axis=1)
    sine = np.concatenate([-np.sin(angles), np.sin(angles)], axis=1)
    return cosine.astype(np.float32), sine.astype(np.float32)


def pick_slots(picks, marks, tokens):
    count = picks.shape[0]
    _, seq_len, wide = tokens.shape
    group = min(4, count)

    def body(pick, mark, x, out):
        first = pl.program_id(0) * group
        for j in range(group):
            out[j, :, :wide] = x[pick[first + j]]
            value = mark[first + j].astype(jnp.float32)
            out[j, :, wide:] = jnp.full((seq_len, HEAD_SIZE), value, jnp.float32).astype(out.dtype)

    return pl.pallas_call(
        body,
        out_shape=jax.ShapeDtypeStruct((count, seq_len, wide + HEAD_SIZE), tokens.dtype),
        grid_spec=pltpu.PrefetchScalarGridSpec(
            num_scalar_prefetch=2,
            grid=(count // group,),
            in_specs=[pl.BlockSpec(tokens.shape, lambda i, *_: (0, 0, 0))],
            out_specs=pl.BlockSpec((group, seq_len, wide + HEAD_SIZE), lambda i, *_: (i, 0, 0)),
        ),
        compiler_params=pltpu.CompilerParams(vmem_limit_bytes=32 << 20),
    )(picks, marks, tokens)


def down_project(received, down):
    rows, lanes = received.shape
    adapters, outs, wide = down.shape
    block = min(256, rows)

    def body(x, w, out):
        features = x[:, :wide]
        mark = x[:, wide : wide + 1].astype(jnp.float32)
        total = jnp.zeros((block, outs), jnp.float32)
        for a in range(adapters):
            one = lax.dot_general(
                features, w[a], (((1,), (1,)), ((), ())), preferred_element_type=jnp.float32
            )
            total = jnp.where(mark == float(a), one, total)
        out[...] = total.astype(jnp.bfloat16)

    return pl.pallas_call(
        body,
        out_shape=jax.ShapeDtypeStruct((rows, outs), jnp.bfloat16),
        grid=(rows // block,),
        in_specs=[
            pl.BlockSpec((block, lanes), lambda i: (i, 0)),
            pl.BlockSpec((adapters, outs, wide), lambda i: (0, 0, 0)),
        ],
        out_specs=pl.BlockSpec((block, outs), lambda i: (i, 0)),
        compiler_params=pltpu.CompilerParams(vmem_limit_bytes=32 << 20),
        cost_estimate=pl.CostEstimate(
            flops=2 * rows * outs * adapters * wide, bytes_accessed=9 << 20, transcendentals=0
        ),
    )(received, down)


def up_project(shrink, received, up_query, up_key, up_value):
    rows, outs = shrink.shape
    adapters, rank, query_cols = up_query.shape
    wide = received.shape[1] - HEAD_SIZE
    block = min(256, rows)
    cols = query_cols + 2 * HEAD_SIZE

    def body(low, marks, wq, wk, wv, out):
        mark = marks[:, :1].astype(jnp.float32)
        start = 0
        for side, w in enumerate((wq, wk, wv)):
            width = w.shape[2]
            part = low[:, side * rank : (side + 1) * rank].astype(jnp.float32)
            total = jnp.zeros((block, width), jnp.float32)
            for a in range(adapters):
                mine = jnp.where(mark == float(a), part, 0.0).astype(jnp.bfloat16)
                total += jnp.dot(mine, w[a], preferred_element_type=jnp.float32)
            out[:, start : start + width] = (adapter_scale * total).astype(jnp.bfloat16)
            start += width

    whole = lambda w: pl.BlockSpec(w.shape, lambda i: (0, 0, 0))
    return pl.pallas_call(
        body,
        out_shape=jax.ShapeDtypeStruct((rows, cols), jnp.bfloat16),
        grid=(rows // block,),
        in_specs=[
            pl.BlockSpec((block, outs), lambda i: (i, 0)),
            pl.BlockSpec((block, HEAD_SIZE), lambda i: (i, wide // HEAD_SIZE)),
            whole(up_query),
            whole(up_key),
            whole(up_value),
        ],
        out_specs=pl.BlockSpec((block, cols), lambda i: (i, 0)),
        compiler_params=pltpu.CompilerParams(vmem_limit_bytes=32 << 20),
        cost_estimate=pl.CostEstimate(
            flops=2 * rows * rank * adapters * cols, bytes_accessed=4 << 20, transcendentals=0
        ),
    )(shrink, received, up_query, up_key, up_value)


def attend_kernel(
    seq_len, per_block, heads_here, first, slots, lengths, base, pair, delta, cosine, sine, out
):
    block = first + pl.program_id(0)
    rows = per_block * seq_len
    query_cols = heads_here * HEAD_SIZE
    picked = [slots[block * per_block + j] for j in range(per_block)]
    sizes = [lengths[block * per_block + j] for j in range(per_block)]

    def change(start, width):
        return jnp.concatenate(
            [delta[s, :, start : start + width] for s in picked], axis=0
        ).astype(jnp.float32)

    cos = cosine[...]
    sin = sine[...]

    def rotate(v):
        return (v * cos + pltpu.roll(v, HALF, 1) * sin).astype(jnp.bfloat16)

    sums = pair[0].astype(jnp.float32)
    for t in range(1, pair.shape[0]):
        sums += pair[t].astype(jnp.float32)
    keys_raw = (sums[:, :HEAD_SIZE] + change(query_cols, HEAD_SIZE)).astype(jnp.bfloat16)
    values = (sums[:, HEAD_SIZE:] + change(query_cols + HEAD_SIZE, HEAD_SIZE)).astype(jnp.bfloat16)
    keys = rotate(keys_raw.astype(jnp.float32))
    q_at = lax.broadcasted_iota(jnp.int32, (rows, rows), 0)
    p_at = lax.broadcasted_iota(jnp.int32, (rows, rows), 1)
    p_request = p_at // seq_len
    q_row = lax.broadcasted_iota(jnp.int32, (rows, HEAD_SIZE), 0)
    limit = jnp.zeros((rows, rows), jnp.int32)
    q_limit = jnp.zeros((rows, HEAD_SIZE), jnp.int32)
    for j in range(per_block):
        limit = jnp.where(p_request == j, sizes[j] + j * seq_len, limit)
        q_limit = jnp.where(q_row // seq_len == j, sizes[j] + j * seq_len, q_limit)
    allowed = (p_request == q_at // seq_len) & (p_at <= q_at) & (p_at < limit)
    live = q_row < q_limit
    for h in range(heads_here):
        at = h * HEAD_SIZE
        query = rotate(base[:, at : at + HEAD_SIZE] + change(at, HEAD_SIZE))
        scores = lax.dot_general(
            query, keys, (((1,), (1,)), ((), ())), preferred_element_type=jnp.float32
        ) * (1.0 / math.sqrt(HEAD_SIZE))
        scores = jnp.where(allowed, scores, jnp.float32(-1e30))
        weights = jnp.exp(scores - jnp.max(scores, axis=1, keepdims=True))
        probs = (weights / jnp.sum(weights, axis=1, keepdims=True)).astype(jnp.bfloat16)
        mixed = jnp.dot(probs, values, preferred_element_type=jnp.float32)
        out[:, at : at + HEAD_SIZE] = jnp.where(live, mixed, 0.0).astype(jnp.bfloat16)


def attend(slots, lengths, base, pair, delta, seq_len, start, tok_rows, earlier):
    base_rows, query_cols = base.shape
    per_block = max(1, HEAD_SIZE // seq_len)
    rows = per_block * seq_len
    first = start // rows
    cosine, sine = rope_tables(seq_len, rows)
    whole = lambda shape: pl.BlockSpec(shape, lambda i, *_: (0,) * len(shape))
    carried = [] if earlier is None else [earlier]

    def body(*refs):
        kept = refs[:7] + refs[7 + len(carried) :]
        attend_kernel(seq_len, per_block, query_cols // HEAD_SIZE, first, *kept)

    return pl.pallas_call(
        body,
        out_shape=jax.ShapeDtypeStruct((tok_rows, query_cols), jnp.bfloat16),
        grid_spec=pltpu.PrefetchScalarGridSpec(
            num_scalar_prefetch=2,
            grid=(base_rows // rows,),
            in_specs=[
                pl.BlockSpec((rows, query_cols), lambda i, *_: (i, 0)),
                pl.BlockSpec(
                    (pair.shape[0], rows, 2 * HEAD_SIZE), lambda i, *_: (0, first + i, 0)
                ),
                whole(delta.shape),
                whole(cosine.shape),
                whole(sine.shape),
            ]
            + [pl.BlockSpec(memory_space=pl.ANY)] * len(carried),
            out_specs=pl.BlockSpec((rows, query_cols), lambda i, *_: (first + i, 0)),
        ),
        input_output_aliases={7: 0} if carried else {},
        compiler_params=pltpu.CompilerParams(vmem_limit_bytes=32 << 20),
        cost_estimate=pl.CostEstimate(
            flops=4 * base_rows * rows * query_cols,
            bytes_accessed=6 * base_rows * query_cols,
            transcendentals=base_rows * query_cols,
        ),
    )(slots, lengths, base, pair, delta, jnp.asarray(cosine), jnp.asarray(sine), *carried)


def shards(
    tokens,
    query_weight,
    key_value_weight,
    adapter_down_tables,
    adapter_up_query,
    adapter_up_key_value,
    request_adapter,
    request_token_length,
    adapter_table_row,
):
    replicas = lax.axis_size("rep")
    tp_count = lax.axis_size("tp")
    tp_here = lax.axis_index("tp")
    tok_rows, feat_local = tokens.shape
    query_cols = query_weight.shape[1]
    pair_total = key_value_weight.shape[1]
    local_rows = adapter_down_tables.shape[0]
    rank = adapter_up_query.shape[1]
    requests_here = request_adapter.shape[0]
    seq_len = tok_rows // requests_here
    capacity = max(1, 2 * requests_here // replicas)
    slot_count = replicas * capacity
    kv_heads = pair_total // (2 * HEAD_SIZE)
    sharing = tp_count // kv_heads

    match = request_adapter[:, None] == jnp.arange(adapter_table_row.shape[0], dtype=jnp.int32)
    homes = jnp.sum(jnp.where(match, adapter_table_row[None, :], 0), axis=1)
    owners = homes // local_rows
    pos = jnp.arange(requests_here, dtype=jnp.int32)
    earlier = (owners[:, None] == owners[None, :]) & (pos[None, :] < pos[:, None])
    slot_ids = owners * capacity + jnp.sum(earlier.astype(jnp.int32), axis=1)
    slot_at = jnp.arange(slot_count, dtype=jnp.int32)
    taken = slot_ids[None, :] == slot_at[:, None]
    picks = jnp.sum(jnp.where(taken, pos, 0), axis=1)
    slot_local = jnp.sum(jnp.where(taken, (homes % local_rows)[None, :], 0), axis=1)

    send = pick_slots(picks, slot_local, tokens.reshape(requests_here, seq_len, feat_local))
    received = lax.all_to_all(send, "rep", split_axis=0, concat_axis=0, tiled=True)
    received = received.reshape(slot_count * seq_len, feat_local + HEAD_SIZE)

    base_pair = jnp.dot(tokens, key_value_weight, preferred_element_type=jnp.float32)
    base_pair = base_pair.astype(jnp.bfloat16)
    side = kv_heads * HEAD_SIZE
    portion = adapter_up_key_value.shape[2]
    flat_up = adapter_up_key_value.reshape(local_rows * rank, portion)
    fold = local_rows * rank // 2
    pieces = []
    for t in range(tp_count):
        at = (t // sharing) * HEAD_SIZE
        up = flat_up[:, at % portion : at % portion + HEAD_SIZE]
        pieces.append(
            jnp.concatenate(
                [
                    jnp.concatenate([base_pair[:, at : at + HEAD_SIZE], up[:fold]], axis=0),
                    jnp.concatenate(
                        [base_pair[:, side + at : side + at + HEAD_SIZE], up[fold:]], axis=0
                    ),
                ],
                axis=1,
            )
        )
    swapped = lax.all_to_all(jnp.stack(pieces), "tp", split_axis=0, concat_axis=0, tiled=True)
    head = tp_here // sharing

    def up_of(column):
        both = lax.dynamic_index_in_dim(swapped, column // portion, 0, keepdims=False)[tok_rows:]
        both = jnp.concatenate([both[:, :HEAD_SIZE], both[:, HEAD_SIZE:]], axis=0)
        return both.reshape(local_rows, rank, HEAD_SIZE)

    up_key = up_of(head * HEAD_SIZE)
    up_value = up_of(side + head * HEAD_SIZE)

    early = tok_rows * 3 // 4
    weight = query_weight.reshape(tp_count, feat_local, query_cols)

    def project(gathered):
        return jnp.einsum("tnf,tfc->nc", gathered, weight, preferred_element_type=jnp.float32)

    first = lax.all_gather(tokens[:early], "tp", axis=0, tiled=False)
    late_rows, received = lax.optimization_barrier((tokens[early:], received))
    second = lax.all_gather(late_rows, "tp", axis=0, tiled=False)

    partial = down_project(received, adapter_down_tables)
    partial = partial.reshape(tp_count, slot_count * seq_len // tp_count, 3 * rank)
    parts = lax.all_to_all(partial, "tp", split_axis=0, concat_axis=0, tiled=True)
    total = parts[0].astype(jnp.float32)
    for t in range(1, tp_count):
        total = total + parts[t].astype(jnp.float32)
    own = jnp.broadcast_to(total.astype(jnp.bfloat16)[None], partial.shape)
    shrink = lax.all_to_all(own, "tp", split_axis=0, concat_axis=0, tiled=True)
    shrink = shrink.reshape(slot_count * seq_len, 3 * rank)

    delta = up_project(shrink, received, adapter_up_query, up_key, up_value)
    returned = lax.all_to_all(
        delta.reshape(slot_count, seq_len, delta.shape[1]),
        "rep",
        split_axis=0,
        concat_axis=0,
        tiled=True,
    )
    fixed = (swapped, returned, seq_len)
    out = attend(slot_ids, request_token_length, project(first), *fixed, 0, tok_rows, None)
    second, out = lax.optimization_barrier((second, out))
    return attend(slot_ids, request_token_length, project(second), *fixed, early, tok_rows, out)


def solution(mesh):
    placed = (
        P("rep", "tp"),
        P(None, "tp"),
        P("tp", None),
        P("rep", None, "tp"),
        P("rep", None, "tp"),
        P("rep", None, "tp"),
        P("rep"),
        P("rep"),
        P(),
    )
    return jax.shard_map(
        shards, mesh=mesh, in_specs=placed, out_specs=P("rep", "tp"), check_vma=False
    )
```

```python
import math

import jax
import jax.numpy as jnp
import numpy as np
from jax import lax
from jax.experimental import pallas as pl
from jax.experimental.pallas import tpu as pltpu
from jax.sharding import PartitionSpec as P

HEAD_SIZE = 128
HALF = HEAD_SIZE // 2

adapter_scale = 0.5
rope_theta = 500000.0


def rope_tables(seq_len, rows):
    frequency = np.float64(rope_theta) ** (-(np.arange(HALF, dtype=np.float64) * 2.0 / HEAD_SIZE))
    angles = (np.arange(rows) % seq_len).astype(np.float64)[:, None] * frequency[None, :]
    cosine = np.concatenate([np.cos(angles), np.cos(angles)], axis=1)
    sine = np.concatenate([-np.sin(angles), np.sin(angles)], axis=1)
    return cosine.astype(np.float32), sine.astype(np.float32)


def pick_slots(picks, marks, tokens):
    count = picks.shape[0]
    _, seq_len, wide = tokens.shape
    group = min(4, count)

    def body(pick, mark, x, out):
        first = pl.program_id(0) * group
        for j in range(group):
            out[j, :, :wide] = x[pick[first + j]]
            value = mark[first + j].astype(jnp.float32)
            out[j, :, wide:] = jnp.full((seq_len, HEAD_SIZE), value, jnp.float32).astype(out.dtype)

    return pl.pallas_call(
        body,
        out_shape=jax.ShapeDtypeStruct((count, seq_len, wide + HEAD_SIZE), tokens.dtype),
        grid_spec=pltpu.PrefetchScalarGridSpec(
            num_scalar_prefetch=2,
            grid=(count // group,),
            in_specs=[pl.BlockSpec(tokens.shape, lambda i, *_: (0, 0, 0))],
            out_specs=pl.BlockSpec((group, seq_len, wide + HEAD_SIZE), lambda i, *_: (i, 0, 0)),
        ),
        compiler_params=pltpu.CompilerParams(vmem_limit_bytes=32 << 20),
    )(picks, marks, tokens)


def down_project(received, down):
    rows, lanes = received.shape
    adapters, outs, wide = down.shape
    block = min(256, rows)

    def body(x, w, out):
        features = x[:, :wide]
        mark = x[:, wide : wide + 1].astype(jnp.float32)
        total = jnp.zeros((block, outs), jnp.float32)
        for a in range(adapters):
            one = lax.dot_general(
                features, w[a], (((1,), (1,)), ((), ())), preferred_element_type=jnp.float32
            )
            total = jnp.where(mark == float(a), one, total)
        out[...] = total.astype(jnp.bfloat16)

    return pl.pallas_call(
        body,
        out_shape=jax.ShapeDtypeStruct((rows, outs), jnp.bfloat16),
        grid=(rows // block,),
        in_specs=[
            pl.BlockSpec((block, lanes), lambda i: (i, 0)),
            pl.BlockSpec((adapters, outs, wide), lambda i: (0, 0, 0)),
        ],
        out_specs=pl.BlockSpec((block, outs), lambda i: (i, 0)),
        compiler_params=pltpu.CompilerParams(vmem_limit_bytes=32 << 20),
        cost_estimate=pl.CostEstimate(
            flops=2 * rows * outs * adapters * wide, bytes_accessed=9 << 20, transcendentals=0
        ),
    )(received, down)


def up_project(shrink, received, up_query, up_key, up_value):
    rows, outs = shrink.shape
    adapters, rank, query_cols = up_query.shape
    wide = received.shape[1] - HEAD_SIZE
    block = min(256, rows)
    cols = query_cols + 2 * HEAD_SIZE

    def body(low, marks, wq, wk, wv, out):
        mark = marks[:, :1].astype(jnp.float32)
        start = 0
        for side, w in enumerate((wq, wk, wv)):
            width = w.shape[2]
            part = low[:, side * rank : (side + 1) * rank].astype(jnp.float32)
            total = jnp.zeros((block, width), jnp.float32)
            for a in range(adapters):
                mine = jnp.where(mark == float(a), part, 0.0).astype(jnp.bfloat16)
                total += jnp.dot(mine, w[a], preferred_element_type=jnp.float32)
            out[:, start : start + width] = (adapter_scale * total).astype(jnp.bfloat16)
            start += width

    whole = lambda w: pl.BlockSpec(w.shape, lambda i: (0, 0, 0))
    return pl.pallas_call(
        body,
        out_shape=jax.ShapeDtypeStruct((rows, cols), jnp.bfloat16),
        grid=(rows // block,),
        in_specs=[
            pl.BlockSpec((block, outs), lambda i: (i, 0)),
            pl.BlockSpec((block, HEAD_SIZE), lambda i: (i, wide // HEAD_SIZE)),
            whole(up_query),
            whole(up_key),
            whole(up_value),
        ],
        out_specs=pl.BlockSpec((block, cols), lambda i: (i, 0)),
        compiler_params=pltpu.CompilerParams(vmem_limit_bytes=32 << 20),
        cost_estimate=pl.CostEstimate(
            flops=2 * rows * rank * adapters * cols, bytes_accessed=4 << 20, transcendentals=0
        ),
    )(shrink, received, up_query, up_key, up_value)


def attend_kernel(
    seq_len, per_block, heads_here, first, slots, lengths, base, pair, delta, cosine, sine, out
):
    block = first + pl.program_id(0)
    rows = per_block * seq_len
    query_cols = heads_here * HEAD_SIZE
    picked = [slots[block * per_block + j] for j in range(per_block)]
    sizes = [lengths[block * per_block + j] for j in range(per_block)]

    def change(start, width):
        return jnp.concatenate(
            [delta[s, :, start : start + width] for s in picked], axis=0
        ).astype(jnp.float32)

    cos = cosine[...]
    sin = sine[...]

    def rotate(v):
        return (v * cos + pltpu.roll(v, HALF, 1) * sin).astype(jnp.bfloat16)

    sums = pair[...]
    keys_raw = (sums[:, :HEAD_SIZE] + change(query_cols, HEAD_SIZE)).astype(jnp.bfloat16)
    values = (sums[:, HEAD_SIZE:] + change(query_cols + HEAD_SIZE, HEAD_SIZE)).astype(jnp.bfloat16)
    keys = rotate(keys_raw.astype(jnp.float32))
    q_at = lax.broadcasted_iota(jnp.int32, (rows, rows), 0)
    p_at = lax.broadcasted_iota(jnp.int32, (rows, rows), 1)
    p_request = p_at // seq_len
    q_row = lax.broadcasted_iota(jnp.int32, (rows, HEAD_SIZE), 0)
    limit = jnp.zeros((rows, rows), jnp.int32)
    q_limit = jnp.zeros((rows, HEAD_SIZE), jnp.int32)
    for j in range(per_block):
        limit = jnp.where(p_request == j, sizes[j] + j * seq_len, limit)
        q_limit = jnp.where(q_row // seq_len == j, sizes[j] + j * seq_len, q_limit)
    allowed = (p_request == q_at // seq_len) & (p_at <= q_at) & (p_at < limit)
    live = q_row < q_limit
    for h in range(heads_here):
        at = h * HEAD_SIZE
        query = rotate(base[:, at : at + HEAD_SIZE] + change(at, HEAD_SIZE))
        scores = lax.dot_general(
            query, keys, (((1,), (1,)), ((), ())), preferred_element_type=jnp.float32
        ) * (1.0 / math.sqrt(HEAD_SIZE))
        scores = jnp.where(allowed, scores, jnp.float32(-1e30))
        weights = jnp.exp(scores - jnp.max(scores, axis=1, keepdims=True))
        probs = (weights / jnp.sum(weights, axis=1, keepdims=True)).astype(jnp.bfloat16)
        mixed = jnp.dot(probs, values, preferred_element_type=jnp.float32)
        out[:, at : at + HEAD_SIZE] = jnp.where(live, mixed, 0.0).astype(jnp.bfloat16)


def attend(slots, lengths, base, pair, delta, seq_len, start, tok_rows, earlier):
    base_rows, query_cols = base.shape
    per_block = max(1, HEAD_SIZE // seq_len)
    rows = per_block * seq_len
    first = start // rows
    cosine, sine = rope_tables(seq_len, rows)
    whole = lambda shape: pl.BlockSpec(shape, lambda i, *_: (0,) * len(shape))
    carried = [] if earlier is None else [earlier]

    def body(*refs):
        kept = refs[:7] + refs[7 + len(carried) :]
        attend_kernel(seq_len, per_block, query_cols // HEAD_SIZE, first, *kept)

    return pl.pallas_call(
        body,
        out_shape=jax.ShapeDtypeStruct((tok_rows, query_cols), jnp.bfloat16),
        grid_spec=pltpu.PrefetchScalarGridSpec(
            num_scalar_prefetch=2,
            grid=(base_rows // rows,),
            in_specs=[
                pl.BlockSpec((rows, query_cols), lambda i, *_: (i, 0)),
                pl.BlockSpec((rows, 2 * HEAD_SIZE), lambda i, *_: (first + i, 0)),
                whole(delta.shape),
                whole(cosine.shape),
                whole(sine.shape),
            ]
            + [pl.BlockSpec(memory_space=pl.ANY)] * len(carried),
            out_specs=pl.BlockSpec((rows, query_cols), lambda i, *_: (first + i, 0)),
        ),
        input_output_aliases={7: 0} if carried else {},
        compiler_params=pltpu.CompilerParams(vmem_limit_bytes=32 << 20),
        cost_estimate=pl.CostEstimate(
            flops=4 * base_rows * rows * query_cols,
            bytes_accessed=6 * base_rows * query_cols,
            transcendentals=base_rows * query_cols,
        ),
    )(slots, lengths, base, pair, delta, jnp.asarray(cosine), jnp.asarray(sine), *carried)


def shards(
    tokens,
    query_weight,
    key_value_weight,
    adapter_down_tables,
    adapter_up_query,
    adapter_up_key_value,
    request_adapter,
    request_token_length,
    adapter_table_row,
):
    replicas = lax.axis_size("rep")
    tp_count = lax.axis_size("tp")
    tp_here = lax.axis_index("tp")
    tok_rows, feat_local = tokens.shape
    query_cols = query_weight.shape[1]
    pair_total = key_value_weight.shape[1]
    local_rows = adapter_down_tables.shape[0]
    rank = adapter_up_query.shape[1]
    requests_here = request_adapter.shape[0]
    seq_len = tok_rows // requests_here
    capacity = max(1, 2 * requests_here // replicas)
    slot_count = replicas * capacity
    kv_heads = pair_total // (2 * HEAD_SIZE)
    sharing = tp_count // kv_heads

    match = request_adapter[:, None] == jnp.arange(adapter_table_row.shape[0], dtype=jnp.int32)
    homes = jnp.sum(jnp.where(match, adapter_table_row[None, :], 0), axis=1)
    owners = homes // local_rows
    pos = jnp.arange(requests_here, dtype=jnp.int32)
    earlier = (owners[:, None] == owners[None, :]) & (pos[None, :] < pos[:, None])
    slot_ids = owners * capacity + jnp.sum(earlier.astype(jnp.int32), axis=1)
    slot_at = jnp.arange(slot_count, dtype=jnp.int32)
    taken = slot_ids[None, :] == slot_at[:, None]
    picks = jnp.sum(jnp.where(taken, pos, 0), axis=1)
    slot_local = jnp.sum(jnp.where(taken, (homes % local_rows)[None, :], 0), axis=1)

    send = pick_slots(picks, slot_local, tokens.reshape(requests_here, seq_len, feat_local))
    received = lax.all_to_all(send, "rep", split_axis=0, concat_axis=0, tiled=True)
    received = received.reshape(slot_count * seq_len, feat_local + HEAD_SIZE)

    base_pair = jnp.dot(tokens, key_value_weight, preferred_element_type=jnp.float32)
    base_pair = base_pair.astype(jnp.bfloat16)
    side = kv_heads * HEAD_SIZE
    portion = adapter_up_key_value.shape[2]
    flat_up = adapter_up_key_value.reshape(local_rows * rank, portion)
    fold = local_rows * rank // 2
    pieces = []
    for t in range(tp_count):
        at = (t // sharing) * HEAD_SIZE
        up = flat_up[:, at % portion : at % portion + HEAD_SIZE]
        pieces.append(
            jnp.concatenate(
                [
                    jnp.concatenate([base_pair[:, at : at + HEAD_SIZE], up[:fold]], axis=0),
                    jnp.concatenate(
                        [base_pair[:, side + at : side + at + HEAD_SIZE], up[fold:]], axis=0
                    ),
                ],
                axis=1,
            )
        )
    pieces = jnp.stack(pieces)
    arrived = []
    for step in range(tp_count):
        piece = lax.dynamic_index_in_dim(pieces, (tp_here + step) % tp_count, 0, keepdims=False)
        if step:
            ring = [(t, (t + step) % tp_count) for t in range(tp_count)]
            piece = lax.ppermute(piece, "tp", ring)
        arrived.append(piece)
    pair_here = arrived[0][:tok_rows].astype(jnp.float32)
    for piece in arrived[1:]:
        pair_here = pair_here + piece[:tok_rows].astype(jnp.float32)
    ups = jnp.stack([piece[tok_rows:] for piece in arrived])
    head = tp_here // sharing

    def up_of(column):
        step = (tp_here - column // portion + tp_count) % tp_count
        both = lax.dynamic_index_in_dim(ups, step, 0, keepdims=False)
        both = jnp.concatenate([both[:, :HEAD_SIZE], both[:, HEAD_SIZE:]], axis=0)
        return both.reshape(local_rows, rank, HEAD_SIZE)

    up_key = up_of(head * HEAD_SIZE)
    up_value = up_of(side + head * HEAD_SIZE)

    early = tok_rows * 3 // 4
    weight = query_weight.reshape(tp_count, feat_local, query_cols)

    def project(gathered):
        return jnp.einsum("tnf,tfc->nc", gathered, weight, preferred_element_type=jnp.float32)

    first = lax.all_gather(tokens[:early], "tp", axis=0, tiled=False)
    late_rows, received = lax.optimization_barrier((tokens[early:], received))
    second = lax.all_gather(late_rows, "tp", axis=0, tiled=False)

    partial = down_project(received, adapter_down_tables)
    partial = partial.reshape(tp_count, slot_count * seq_len // tp_count, 3 * rank)
    parts = lax.all_to_all(partial, "tp", split_axis=0, concat_axis=0, tiled=True)
    total = parts[0].astype(jnp.float32)
    for t in range(1, tp_count):
        total = total + parts[t].astype(jnp.float32)
    own = jnp.broadcast_to(total.astype(jnp.bfloat16)[None], partial.shape)
    shrink = lax.all_to_all(own, "tp", split_axis=0, concat_axis=0, tiled=True)
    shrink = shrink.reshape(slot_count * seq_len, 3 * rank)

    delta = up_project(shrink, received, adapter_up_query, up_key, up_value)
    returned = lax.all_to_all(
        delta.reshape(slot_count, seq_len, delta.shape[1]),
        "rep",
        split_axis=0,
        concat_axis=0,
        tiled=True,
    )
    fixed = (pair_here, returned, seq_len)
    out = attend(slot_ids, request_token_length, project(first), *fixed, 0, tok_rows, None)
    second, out = lax.optimization_barrier((second, out))
    return attend(slot_ids, request_token_length, project(second), *fixed, early, tok_rows, out)


def solution(mesh):
    placed = (
        P("rep", "tp"),
        P(None, "tp"),
        P("tp", None),
        P("rep", None, "tp"),
        P("rep", None, "tp"),
        P("rep", None, "tp"),
        P("rep"),
        P("rep"),
        P(),
    )
    return jax.shard_map(
        shards, mesh=mesh, in_specs=placed, out_specs=P("rep", "tp"), check_vma=False
    )
```

```python
import math

import jax
import jax.numpy as jnp
import numpy as np
from jax import lax
from jax.experimental import pallas as pl
from jax.experimental.pallas import tpu as pltpu
from jax.sharding import PartitionSpec as P

HEAD_SIZE = 128
HALF = HEAD_SIZE // 2

adapter_scale = 0.5
rope_theta = 500000.0


def rope_tables(seq_len, rows):
    frequency = np.float64(rope_theta) ** (-(np.arange(HALF, dtype=np.float64) * 2.0 / HEAD_SIZE))
    angles = (np.arange(rows) % seq_len).astype(np.float64)[:, None] * frequency[None, :]
    cosine = np.concatenate([np.cos(angles), np.cos(angles)], axis=1)
    sine = np.concatenate([-np.sin(angles), np.sin(angles)], axis=1)
    return cosine.astype(np.float32), sine.astype(np.float32)


def pick_slots(picks, marks, tokens):
    count = picks.shape[0]
    _, seq_len, wide = tokens.shape
    group = min(4, count)

    def body(pick, mark, x, out):
        first = pl.program_id(0) * group
        for j in range(group):
            out[j, :, :wide] = x[pick[first + j]]
            value = mark[first + j].astype(jnp.float32)
            out[j, :, wide:] = jnp.full((seq_len, HEAD_SIZE), value, jnp.float32).astype(out.dtype)

    return pl.pallas_call(
        body,
        out_shape=jax.ShapeDtypeStruct((count, seq_len, wide + HEAD_SIZE), tokens.dtype),
        grid_spec=pltpu.PrefetchScalarGridSpec(
            num_scalar_prefetch=2,
            grid=(count // group,),
            in_specs=[pl.BlockSpec(tokens.shape, lambda i, *_: (0, 0, 0))],
            out_specs=pl.BlockSpec((group, seq_len, wide + HEAD_SIZE), lambda i, *_: (i, 0, 0)),
        ),
        compiler_params=pltpu.CompilerParams(vmem_limit_bytes=32 << 20),
    )(picks, marks, tokens)


def down_project(received, down):
    rows, lanes = received.shape
    adapters, outs, wide = down.shape
    block = min(256, rows)

    def body(x, w, out):
        features = x[:, :wide]
        mark = x[:, wide : wide + 1].astype(jnp.float32)
        total = jnp.zeros((block, outs), jnp.float32)
        for a in range(adapters):
            one = lax.dot_general(
                features, w[a], (((1,), (1,)), ((), ())), preferred_element_type=jnp.float32
            )
            total = jnp.where(mark == float(a), one, total)
        out[...] = total.astype(jnp.bfloat16)

    return pl.pallas_call(
        body,
        out_shape=jax.ShapeDtypeStruct((rows, outs), jnp.bfloat16),
        grid=(rows // block,),
        in_specs=[
            pl.BlockSpec((block, lanes), lambda i: (i, 0)),
            pl.BlockSpec((adapters, outs, wide), lambda i: (0, 0, 0)),
        ],
        out_specs=pl.BlockSpec((block, outs), lambda i: (i, 0)),
        compiler_params=pltpu.CompilerParams(vmem_limit_bytes=32 << 20),
        cost_estimate=pl.CostEstimate(
            flops=2 * rows * outs * adapters * wide, bytes_accessed=9 << 20, transcendentals=0
        ),
    )(received, down)


def up_project(shrink, received, up_query, up_key, up_value):
    rows, outs = shrink.shape
    adapters, rank, query_cols = up_query.shape
    wide = received.shape[1] - HEAD_SIZE
    block = min(256, rows)
    cols = query_cols + 2 * HEAD_SIZE

    def body(low, marks, wq, wk, wv, out):
        mark = marks[:, :1].astype(jnp.float32)
        start = 0
        for side, w in enumerate((wq, wk, wv)):
            width = w.shape[2]
            part = low[:, side * rank : (side + 1) * rank].astype(jnp.float32)
            total = jnp.zeros((block, width), jnp.float32)
            for a in range(adapters):
                mine = jnp.where(mark == float(a), part, 0.0).astype(jnp.bfloat16)
                total += jnp.dot(mine, w[a], preferred_element_type=jnp.float32)
            out[:, start : start + width] = (adapter_scale * total).astype(jnp.bfloat16)
            start += width

    whole = lambda w: pl.BlockSpec(w.shape, lambda i: (0, 0, 0))
    return pl.pallas_call(
        body,
        out_shape=jax.ShapeDtypeStruct((rows, cols), jnp.bfloat16),
        grid=(rows // block,),
        in_specs=[
            pl.BlockSpec((block, outs), lambda i: (i, 0)),
            pl.BlockSpec((block, HEAD_SIZE), lambda i: (i, wide // HEAD_SIZE)),
            whole(up_query),
            whole(up_key),
            whole(up_value),
        ],
        out_specs=pl.BlockSpec((block, cols), lambda i: (i, 0)),
        compiler_params=pltpu.CompilerParams(vmem_limit_bytes=32 << 20),
        cost_estimate=pl.CostEstimate(
            flops=2 * rows * rank * adapters * cols, bytes_accessed=4 << 20, transcendentals=0
        ),
    )(shrink, received, up_query, up_key, up_value)


def attend_kernel(
    seq_len, per_block, heads_here, first, slots, lengths, base, pair, delta, cosine, sine, out
):
    block = first + pl.program_id(0)
    rows = per_block * seq_len
    query_cols = heads_here * HEAD_SIZE
    picked = [slots[block * per_block + j] for j in range(per_block)]
    sizes = [lengths[block * per_block + j] for j in range(per_block)]

    def change(start, width):
        return jnp.concatenate(
            [delta[s, :, start : start + width] for s in picked], axis=0
        ).astype(jnp.float32)

    cos = cosine[...]
    sin = sine[...]

    def rotate(v):
        return (v * cos + pltpu.roll(v, HALF, 1) * sin).astype(jnp.bfloat16)

    sums = pair[...]
    keys_raw = (sums[:, :HEAD_SIZE] + change(query_cols, HEAD_SIZE)).astype(jnp.bfloat16)
    values = (sums[:, HEAD_SIZE:] + change(query_cols + HEAD_SIZE, HEAD_SIZE)).astype(jnp.bfloat16)
    keys = rotate(keys_raw.astype(jnp.float32))
    q_at = lax.broadcasted_iota(jnp.int32, (rows, rows), 0)
    p_at = lax.broadcasted_iota(jnp.int32, (rows, rows), 1)
    p_request = p_at // seq_len
    q_row = lax.broadcasted_iota(jnp.int32, (rows, HEAD_SIZE), 0)
    limit = jnp.zeros((rows, rows), jnp.int32)
    q_limit = jnp.zeros((rows, HEAD_SIZE), jnp.int32)
    for j in range(per_block):
        limit = jnp.where(p_request == j, sizes[j] + j * seq_len, limit)
        q_limit = jnp.where(q_row // seq_len == j, sizes[j] + j * seq_len, q_limit)
    allowed = (p_request == q_at // seq_len) & (p_at <= q_at) & (p_at < limit)
    live = q_row < q_limit
    for h in range(heads_here):
        at = h * HEAD_SIZE
        query = rotate(base[:, at : at + HEAD_SIZE] + change(at, HEAD_SIZE))
        scores = lax.dot_general(
            query, keys, (((1,), (1,)), ((), ())), preferred_element_type=jnp.float32
        ) * (1.0 / math.sqrt(HEAD_SIZE))
        scores = jnp.where(allowed, scores, jnp.float32(-1e30))
        weights = jnp.exp(scores - jnp.max(scores, axis=1, keepdims=True))
        probs = (weights / jnp.sum(weights, axis=1, keepdims=True)).astype(jnp.bfloat16)
        mixed = jnp.dot(probs, values, preferred_element_type=jnp.float32)
        out[:, at : at + HEAD_SIZE] = jnp.where(live, mixed, 0.0).astype(jnp.bfloat16)


def attend(slots, lengths, base, pair, delta, seq_len, start, tok_rows, earlier):
    base_rows, query_cols = base.shape
    per_block = max(1, HEAD_SIZE // seq_len)
    rows = per_block * seq_len
    first = start // rows
    cosine, sine = rope_tables(seq_len, rows)
    whole = lambda shape: pl.BlockSpec(shape, lambda i, *_: (0,) * len(shape))
    carried = [] if earlier is None else [earlier]

    def body(*refs):
        kept = refs[:7] + refs[7 + len(carried) :]
        attend_kernel(seq_len, per_block, query_cols // HEAD_SIZE, first, *kept)

    return pl.pallas_call(
        body,
        out_shape=jax.ShapeDtypeStruct((tok_rows, query_cols), jnp.bfloat16),
        grid_spec=pltpu.PrefetchScalarGridSpec(
            num_scalar_prefetch=2,
            grid=(base_rows // rows,),
            in_specs=[
                pl.BlockSpec((rows, query_cols), lambda i, *_: (i, 0)),
                pl.BlockSpec((rows, 2 * HEAD_SIZE), lambda i, *_: (first + i, 0)),
                whole(delta.shape),
                whole(cosine.shape),
                whole(sine.shape),
            ]
            + [pl.BlockSpec(memory_space=pl.ANY)] * len(carried),
            out_specs=pl.BlockSpec((rows, query_cols), lambda i, *_: (first + i, 0)),
        ),
        input_output_aliases={7: 0} if carried else {},
        compiler_params=pltpu.CompilerParams(vmem_limit_bytes=32 << 20),
        cost_estimate=pl.CostEstimate(
            flops=4 * base_rows * rows * query_cols,
            bytes_accessed=6 * base_rows * query_cols,
            transcendentals=base_rows * query_cols,
        ),
    )(slots, lengths, base, pair, delta, jnp.asarray(cosine), jnp.asarray(sine), *carried)


def shards(
    tokens,
    query_weight,
    key_value_weight,
    adapter_down_tables,
    adapter_up_query,
    adapter_up_key_value,
    request_adapter,
    request_token_length,
    adapter_table_row,
):
    replicas = lax.axis_size("rep")
    tp_count = lax.axis_size("tp")
    tp_here = lax.axis_index("tp")
    tok_rows, feat_local = tokens.shape
    query_cols = query_weight.shape[1]
    pair_total = key_value_weight.shape[1]
    local_rows = adapter_down_tables.shape[0]
    rank = adapter_up_query.shape[1]
    requests_here = request_adapter.shape[0]
    seq_len = tok_rows // requests_here
    capacity = max(1, 2 * requests_here // replicas)
    slot_count = replicas * capacity
    kv_heads = pair_total // (2 * HEAD_SIZE)
    sharing = tp_count // kv_heads

    match = request_adapter[:, None] == jnp.arange(adapter_table_row.shape[0], dtype=jnp.int32)
    homes = jnp.sum(jnp.where(match, adapter_table_row[None, :], 0), axis=1)
    owners = homes // local_rows
    pos = jnp.arange(requests_here, dtype=jnp.int32)
    earlier = (owners[:, None] == owners[None, :]) & (pos[None, :] < pos[:, None])
    slot_ids = owners * capacity + jnp.sum(earlier.astype(jnp.int32), axis=1)
    slot_at = jnp.arange(slot_count, dtype=jnp.int32)
    taken = slot_ids[None, :] == slot_at[:, None]
    picks = jnp.sum(jnp.where(taken, pos, 0), axis=1)
    slot_local = jnp.sum(jnp.where(taken, (homes % local_rows)[None, :], 0), axis=1)

    send = pick_slots(picks, slot_local, tokens.reshape(requests_here, seq_len, feat_local))
    received = lax.all_to_all(send, "rep", split_axis=0, concat_axis=0, tiled=True)
    received = received.reshape(slot_count * seq_len, feat_local + HEAD_SIZE)

    base_pair = jnp.dot(tokens, key_value_weight, preferred_element_type=jnp.float32)
    base_pair = base_pair.astype(jnp.bfloat16)
    side = kv_heads * HEAD_SIZE
    portion = adapter_up_key_value.shape[2]
    flat_up = adapter_up_key_value.reshape(local_rows * rank, portion)
    fold = local_rows * rank // 2
    pieces = []
    for t in range(tp_count):
        at = (t // sharing) * HEAD_SIZE
        up = flat_up[:, at % portion : at % portion + HEAD_SIZE]
        pieces.append(
            jnp.concatenate(
                [
                    jnp.concatenate([base_pair[:, at : at + HEAD_SIZE], up[:fold]], axis=0),
                    jnp.concatenate(
                        [base_pair[:, side + at : side + at + HEAD_SIZE], up[fold:]], axis=0
                    ),
                ],
                axis=1,
            )
        )
    pieces = jnp.stack(pieces)
    arrived = []
    for step in range(tp_count):
        piece = lax.dynamic_index_in_dim(pieces, (tp_here + step) % tp_count, 0, keepdims=False)
        if step:
            ring = [(t, (t + step) % tp_count) for t in range(tp_count)]
            piece = lax.ppermute(piece, "tp", ring)
        arrived.append(piece)
    pair_here = arrived[0][:tok_rows].astype(jnp.float32)
    for piece in arrived[1:]:
        pair_here = pair_here + piece[:tok_rows].astype(jnp.float32)
    ups = jnp.stack([piece[tok_rows:] for piece in arrived])
    head = tp_here // sharing

    def up_of(column):
        step = (tp_here - column // portion + tp_count) % tp_count
        both = lax.dynamic_index_in_dim(ups, step, 0, keepdims=False)
        both = jnp.concatenate([both[:, :HEAD_SIZE], both[:, HEAD_SIZE:]], axis=0)
        return both.reshape(local_rows, rank, HEAD_SIZE)

    up_key = up_of(head * HEAD_SIZE)
    up_value = up_of(side + head * HEAD_SIZE)

    early = tok_rows * 3 // 4
    weight = query_weight.reshape(tp_count, feat_local, query_cols)

    def project(gathered):
        return jnp.einsum("tnf,tfc->nc", gathered, weight, preferred_element_type=jnp.float32)

    rightward = [(t, t + 1) for t in range(tp_count - 1)]
    leftward = [(t + 1, t) for t in range(tp_count - 1)]

    def line_gather(block):
        from_left, from_right = [block], [block]
        for _ in range(tp_count - 1):
            from_left.append(lax.ppermute(from_left[-1], "tp", rightward))
            from_right.append(lax.ppermute(from_right[-1], "tp", leftward))
        turned = [block] + [from_left[k] + from_right[tp_count - k] for k in range(1, tp_count)]
        order = (tp_here - jnp.arange(tp_count) + tp_count) % tp_count
        return jnp.take(jnp.stack(turned), order, axis=0, mode="clip")

    first = line_gather(tokens[:early])
    second = line_gather(tokens[early:])

    partial = down_project(received, adapter_down_tables)
    partial = partial.reshape(tp_count, slot_count * seq_len // tp_count, 3 * rank)
    parts = lax.all_to_all(partial, "tp", split_axis=0, concat_axis=0, tiled=True)
    total = parts[0].astype(jnp.float32)
    for t in range(1, tp_count):
        total = total + parts[t].astype(jnp.float32)
    own = jnp.broadcast_to(total.astype(jnp.bfloat16)[None], partial.shape)
    shrink = lax.all_to_all(own, "tp", split_axis=0, concat_axis=0, tiled=True)
    shrink = shrink.reshape(slot_count * seq_len, 3 * rank)

    delta = up_project(shrink, received, adapter_up_query, up_key, up_value)
    returned = lax.all_to_all(
        delta.reshape(slot_count, seq_len, delta.shape[1]),
        "rep",
        split_axis=0,
        concat_axis=0,
        tiled=True,
    )
    fixed = (pair_here, returned, seq_len)
    out = attend(slot_ids, request_token_length, project(first), *fixed, 0, tok_rows, None)
    second, out = lax.optimization_barrier((second, out))
    return attend(slot_ids, request_token_length, project(second), *fixed, early, tok_rows, out)


def solution(mesh):
    placed = (
        P("rep", "tp"),
        P(None, "tp"),
        P("tp", None),
        P("rep", None, "tp"),
        P("rep", None, "tp"),
        P("rep", None, "tp"),
        P("rep"),
        P("rep"),
        P(),
    )
    return jax.shard_map(
        shards, mesh=mesh, in_specs=placed, out_specs=P("rep", "tp"), check_vma=False
    )
```
